32 devices in a mesh: segment: 4 (over y, x), gy: 8 (over z, core).
Axes of the slice: x: 2, y: 2, z: 4, core: 2. Of those that a mesh axis runs over, the one named last changes fastest.
Arguments:
- crops: bfloat16 [2, 32, 4, 32, 128], P(None, None, None, 'gy'), may hold values from -6 to 6
- cotangent: bfloat16 [2, 32, 4, 32, 128], P(None, None, None, 'gy'), may hold values from -0.59765625 to 0.59765625
- weights: bfloat16 [4, 2, 27, 32, 32], P('segment'), may hold values from -0.375 to 0.375
Outputs:
- features: bfloat16 [4, 2, 32, 4, 32, 128], P('segment', None, None, None, 'gy')
- weight_grads: float32 [4, 2, 27, 32, 32], P('segment')
- input_grads: float32 [4, 2, 32, 4, 32, 128], P('segment', None, None, None, 'gy')
The draws below stay inside these ranges and needn't reach their ends.
All inputs are finite; a program needn't handle non-finite values.
Results may differ from the reference program's by a relative error of at most 0.025.
Values may be sent and summed in bfloat16 or wider, within the bound.
A program may use at most 128 MiB of HBM per device.

```python
import jax
import jax.numpy as jnp
from jax import lax

C = 32
MICRO = 2
Z = 4
X = 128
Y = 32


def steps_of(rng, dims, split, smallest, high):
    def one(dim, shards_of):
        steps = jax.random.uniform(jax.random.fold_in(jax.random.fold_in(rng, 6), dim), (shards_of,), jnp.float32, smallest / len(split), high / len(split))
        return jnp.repeat(jnp.exp(steps), dims[dim] // shards_of).reshape((-1,) + (1,) * (len(dims) - dim - 1))

    factor_of = one(*split[0])
    for cut in split[1:]:
        factor_of = factor_of * one(*cut)
    return factor_of


def gaussian(rng, shape, scale, most, split=(), held_as=jnp.bfloat16):
    gain = steps_of(rng, shape, split, -0.22, 0.18) if split else 1.0
    drawn = jax.random.normal(rng, shape, jnp.float32) * scale * gain
    return jnp.minimum(jnp.maximum(drawn, -most), most).astype(held_as)


def setup_inputs(seed: int = 0) -> dict:
    key_of = jax.random.split(jax.random.key(seed), 4)
    crops = gaussian(key_of[0], (MICRO, C, Z, Y, X), 1.0, 6.0, ((3, 8),))
    cotangent = gaussian(key_of[1], (MICRO, C, Z, Y, X), 0.1, 0.59765625, ((3, 8),))
    weights = gaussian(key_of[2], (4, 2, 27, C, C), (9 * C) ** -0.5, 0.375, ((0, 4),))
    return {"crops": crops, "cotangent": cotangent, "weights": weights}


def surround(volume):
    return jnp.pad(volume, ((0, 0), (1, 1), (1, 1), (1, 1)))


def slices_of(padded, plane_shift, row_count):
    planes = padded.shape[1] - 2
    across = padded.shape[3] - 2
    return jnp.stack([padded[:, plane_shift:plane_shift + planes, row_shift:row_shift + row_count, side_shift:side_shift + across] for row_shift in range(3) for side_shift in range(3)])


def convolve(padded, kernel, row_count):
    result = None
    for plane_shift in range(3):
        stacked = slices_of(padded, plane_shift, row_count).astype(jnp.float32)
        tap_weights = kernel[9 * plane_shift:9 * plane_shift + 9].astype(jnp.float32)
        contribution = jnp.einsum("tczyx,tco->ozyx", stacked, tap_weights, precision=lax.Precision.HIGHEST)
        result = contribution if result is None else result + contribution
    return result


def kernel_grads(padded, gradient, row_count):
    pieces = []
    for plane_shift in range(3):
        stacked = slices_of(padded, plane_shift, row_count).astype(jnp.float32)
        pieces.append(jnp.einsum("tczyx,ozyx->tco", stacked, gradient.astype(jnp.float32), precision=lax.Precision.HIGHEST))
    return jnp.concatenate(pieces, 0)


def flipped(kernel):
    return jnp.transpose(jnp.flip(kernel, 0), (0, 2, 1))


def slope(preact):
    logistic = jax.nn.sigmoid(preact)
    return logistic * (1.0 + preact * (1.0 - logistic))


def reference(crops, cotangent, weights):
    row_count = crops.shape[3]
    features = []
    input_grads = []
    weight_grads = jnp.zeros(weights.shape, jnp.float32)
    for micro_index in range(MICRO):
        entries = []
        stored = []
        carried = crops[micro_index]
        for section in range(4):
            entering = carried
            entries.append(entering)
            if section >= 2:
                merged = (entering.astype(jnp.float32) + entries[3 - section].astype(jnp.float32)).astype(jnp.bfloat16)
            else:
                merged = entering
            input_pad = surround(merged)
            pre_first = convolve(input_pad, weights[section, 0], row_count)
            hidden_pad = surround(jax.nn.silu(pre_first).astype(jnp.bfloat16))
            pre_second = convolve(hidden_pad, weights[section, 1], row_count)
            carried = jax.nn.silu(pre_second).astype(jnp.bfloat16)
            stored.append((input_pad, pre_first, hidden_pad, pre_second, carried))
        incoming = cotangent[micro_index]
        deltas = [None, None, None, None]
        sums = [None, None, None, None]
        for section in (3, 2, 1, 0):
            input_pad, pre_first, hidden_pad, pre_second, unused_out = stored[section]
            second_delta = (incoming.astype(jnp.float32) * slope(pre_second)).astype(jnp.bfloat16)
            grad_second = kernel_grads(hidden_pad, second_delta, row_count)
            hidden_delta = convolve(surround(second_delta), flipped(weights[section, 1]), row_count)
            first_delta = (hidden_delta * slope(pre_first)).astype(jnp.bfloat16)
            grad_first = kernel_grads(input_pad, first_delta, row_count)
            weight_grads = weight_grads.at[section].add(jnp.stack([grad_first, grad_second]))
            deltas[section] = convolve(surround(first_delta), flipped(weights[section, 0]), row_count).astype(jnp.bfloat16)
            if section == 1:
                sums[1] = deltas[1].astype(jnp.float32) + deltas[2].astype(jnp.float32)
                incoming = sums[1].astype(jnp.bfloat16)
            elif section == 0:
                sums[0] = deltas[0].astype(jnp.float32) + deltas[3].astype(jnp.float32)
            else:
                sums[section] = deltas[section].astype(jnp.float32)
                incoming = deltas[section]
        input_grads.append(jnp.stack(sums))
        features.append(jnp.stack([stored[section][4] for section in range(4)]))
    return jnp.stack(features, 1), weight_grads, jnp.stack(input_grads, 1)
```

```python
import functools

import jax
import jax.numpy as jnp
from jax import lax
from jax.experimental import pallas as pl
from jax.experimental.pallas import tpu as pltpu
from jax.sharding import PartitionSpec as P

HALO = 2


def shifted_fields(value):
    across = value.shape[1]
    lane = lax.broadcasted_iota(jnp.int32, value.shape, 1)
    left = jnp.where(lane == 0, 0.0, pltpu.roll(value, 1, 1))
    right = jnp.where(lane == across - 1, 0.0, pltpu.roll(value, across - 1, 1))
    return [v.astype(jnp.bfloat16) for v in (left, value, right)]


def fill_columns(col, planes_of, planes):
    across = col.shape[-1] // 2
    frame = col.shape[2]
    zero = jnp.zeros((frame, across), jnp.bfloat16)
    for dx in range(3):
        col[dx, 0, :, :across] = zero
        col[dx, planes, :, across:] = zero
    for z in range(planes):
        for dx, field in enumerate(shifted_fields(planes_of(z))):
            col[dx, z + 1, :, :across] = field
            col[dx, z, :, across:] = field


def build_taps(taps, compact, out_rows):
    channels = compact.shape[1]
    frame = taps.shape[2]
    for j in range(9):
        wide = jnp.concatenate(
            [
                compact[j].astype(jnp.float32),
                jnp.zeros((channels, frame - compact.shape[2]), jnp.float32),
            ],
            1,
        )
        for y in range(out_rows):
            moved = wide if y == 0 else pltpu.roll(wide, y * channels, 1)
            taps[j, y * channels : (y + 1) * channels, :] = moved.astype(jnp.bfloat16)


def convolved(taps, col, pair, low, high):
    total = None
    for dz in range(3):
        for dx in range(3):
            part = jnp.dot(
                taps[3 * dz + dx, low:high, :],
                col[dx, 2 * pair + dz],
                preferred_element_type=jnp.float32,
            )
            total = part if total is None else total + part
    return total


def logistic_of(value):
    return 1.0 / (1.0 + jnp.exp(-value))


def row_mask(channels, rows, frame_start, inside_low, inside_high, across):
    row = lax.broadcasted_iota(jnp.int32, (rows * channels, across), 0) // channels + frame_start
    return (row >= inside_low) & (row < inside_high)


def forward_kernel(
    sizes, with_skip, low_ref, mid_ref, high_ref, first_ref, second_ref, *rest
):
    channels, planes, rows, across = sizes
    if with_skip:
        skip_ref, *rest = rest
    (features_ref, next_ref, frame_ref, hidden_ref, slope1_ref, slope2_ref, col, taps) = rest
    gy = lax.axis_index("gy")
    count = lax.axis_size("gy")
    inner = rows + 2
    inside_low = jnp.where(gy == 0, HALO, 0)
    inside_high = jnp.where(gy == count - 1, rows + HALO, rows + 2 * HALO)
    for z in range(planes):
        frame_ref[z, : HALO * channels] = low_ref[z]
        frame_ref[z, HALO * channels : (HALO + rows) * channels] = mid_ref[z]
        frame_ref[z, (HALO + rows) * channels :] = high_ref[z]
    fill_columns(col, lambda z: frame_ref[z].astype(jnp.float32), planes)
    build_taps(taps, first_ref, inner)
    mask = row_mask(channels, inner, 1, inside_low, inside_high, across)
    edge = jnp.zeros((channels, across), jnp.bfloat16)
    for pair in range(planes // 2):
        pre = convolved(taps, col, pair, 0, inner * channels)
        for half in range(2):
            z = 2 * pair + half
            part = pre[:, half * across : (half + 1) * across]
            logistic = logistic_of(part)
            slope1_ref[z] = logistic * (1.0 + part * (1.0 - logistic))
            hidden_ref[z, :channels] = edge
            hidden_ref[z, channels : (inner + 1) * channels] = jnp.where(
                mask, part * logistic, 0.0
            ).astype(jnp.bfloat16)
            hidden_ref[z, (inner + 1) * channels :] = edge
    fill_columns(col, lambda z: hidden_ref[z].astype(jnp.float32), planes)
    build_taps(taps, second_ref, inner)
    for pair in range(planes // 2):
        pre = convolved(taps, col, pair, channels, (rows + 1) * channels)
        for half in range(2):
            z = 2 * pair + half
            part = pre[:, half * across : (half + 1) * across]
            logistic = logistic_of(part)
            slope2_ref[z] = logistic * (1.0 + part * (1.0 - logistic))
            leaving = (part * logistic).astype(jnp.bfloat16)
            features_ref[z] = leaving
            if with_skip:
                leaving = (
                    leaving.astype(jnp.float32) + skip_ref[z].astype(jnp.float32)
                ).astype(jnp.bfloat16)
            next_ref[z] = leaving


def backward_kernel(
    sizes, with_extra, with_next, low_ref, mid_ref, high_ref, first_ref, second_ref, slope1_ref, *rest
):
    channels, planes, rows, across = sizes
    if with_extra:
        extra_ref, *rest = rest
    if with_next:
        slope2_ref, *rest = rest
        (grads_ref, first_delta_ref, next_ref, wide, col, taps) = rest
    else:
        (grads_ref, first_delta_ref, wide, col, taps) = rest
    gy = lax.axis_index("gy")
    count = lax.axis_size("gy")
    inner = rows + 2
    inside_low = jnp.where(gy == 0, HALO, 0)
    inside_high = jnp.where(gy == count - 1, rows + HALO, rows + 2 * HALO)
    for z in range(planes):
        wide[z, : HALO * channels] = low_ref[z]
        wide[z, HALO * channels : (HALO + rows) * channels] = mid_ref[z]
        wide[z, (HALO + rows) * channels :] = high_ref[z]
    fill_columns(col, lambda z: wide[z].astype(jnp.float32), planes)
    build_taps(taps, second_ref, inner)
    mask = row_mask(channels, inner, 1, inside_low, inside_high, across)
    edge = jnp.zeros((channels, across), jnp.bfloat16)
    for pair in range(planes // 2):
        pre = convolved(taps, col, pair, 0, inner * channels)
        for half in range(2):
            z = 2 * pair + half
            part = pre[:, half * across : (half + 1) * across]
            delta = jnp.where(mask, part * slope1_ref[z], 0.0).astype(jnp.bfloat16)
            wide[z, :channels] = edge
            wide[z, channels : (inner + 1) * channels] = delta
            wide[z, (inner + 1) * channels :] = edge
            first_delta_ref[z] = delta[channels : (rows + 1) * channels]
    fill_columns(col, lambda z: wide[z].astype(jnp.float32), planes)
    build_taps(taps, first_ref, inner)
    for pair in range(planes // 2):
        pre = convolved(taps, col, pair, channels, (rows + 1) * channels)
        for half in range(2):
            z = 2 * pair + half
            value = pre[:, half * across : (half + 1) * across].astype(jnp.bfloat16)
            if with_extra:
                value = (
                    value.astype(jnp.float32) + extra_ref[z].astype(jnp.float32)
                ).astype(jnp.bfloat16)
            grads_ref[z] = value
            if with_next:
                next_ref[z] = (value.astype(jnp.float32) * slope2_ref[z]).astype(jnp.bfloat16)


def weight_kernel(sizes, frame_ref, first_ref, hidden_ref, second_ref, out_ref, columns):
    channels, planes, rows, across = sizes
    zero = jnp.zeros((channels, rows * across), jnp.bfloat16)
    for index, (source, delta) in enumerate(((frame_ref, first_ref), (hidden_ref, second_ref))):
        for z in range(planes):
            fields = shifted_fields(source[z].astype(jnp.float32))
            for dx, field in enumerate(fields):
                for dy in range(3):
                    block = jnp.concatenate(
                        [
                            field[(y + 1 + dy) * channels : (y + 2 + dy) * channels]
                            for y in range(rows)
                        ],
                        1,
                    )
                    for dz in range(3):
                        target = z + 1 - dz
                        if 0 <= target < planes:
                            tap = (9 * dz + 3 * dy + dx) * channels
                            columns[
                                tap : tap + channels,
                                target * rows * across : (target + 1) * rows * across,
                            ] = block
        for dz, target in ((0, 0), (2, planes - 1)):
            for tap in range(9 * dz, 9 * dz + 9):
                columns[
                    tap * channels : (tap + 1) * channels,
                    target * rows * across : (target + 1) * rows * across,
                ] = zero
        right = jnp.concatenate(
            [
                delta[z, y * channels : (y + 1) * channels, :]
                for z in range(planes)
                for y in range(rows)
            ],
            1,
        )
        out_ref[index] = lax.dot_general(
            right, columns[...], (((1,), (1,)), ((), ())), preferred_element_type=jnp.float32
        )


def with_halos(block, channels):
    count = lax.axis_size("gy")
    width = HALO * channels
    forward = [(i, i + 1) for i in range(count - 1)]
    backward = [(i + 1, i) for i in range(count - 1)]
    low = lax.ppermute(block[:, -width:], "gy", forward)
    high = lax.ppermute(block[:, :width], "gy", backward)
    return low, block, high


def partner(array, axis, mask):
    return lax.ppermute(array, axis, [(i, i ^ mask) for i in range(lax.axis_size(axis))])


def local(crops, cotangent, weights):
    micro_count, channels, planes, rows, across = crops.shape
    sizes = (channels, planes, rows, across)
    segment = lax.axis_index("segment")
    sections = lax.axis_size("segment")
    micro = segment % 2
    upper = segment >= 2
    inner = rows + 2
    frame = (rows + 2 * HALO) * channels
    spec = pl.BlockSpec(memory_space=pltpu.VMEM)
    bf = lambda *shape: jax.ShapeDtypeStruct(shape, jnp.bfloat16)
    fl = lambda *shape: jax.ShapeDtypeStruct(shape, jnp.float32)
    params = pltpu.CompilerParams(vmem_limit_bytes=48 * 2**20)
    column_scratch = pltpu.VMEM((3, planes + 1, frame, 2 * across), jnp.bfloat16)
    tap_scratch = pltpu.VMEM((9, inner * channels, frame), jnp.bfloat16)

    kernels = weights[0].reshape(2, 3, 3, 3, channels, channels)
    straight = jnp.transpose(kernels, (0, 1, 3, 5, 2, 4))
    turned = jnp.transpose(jnp.flip(kernels, (1, 2, 3)), (0, 1, 3, 4, 2, 5))
    compact = jnp.stack([straight, turned], 1).reshape(2, 2, 9, channels, 3 * channels)
    compact = jnp.pad(compact, ((0, 0),) * 4 + ((0, 128 - 3 * channels),))
    gathered = [compact]
    for step in range(1, sections):
        gathered.append(
            lax.ppermute(
                compact, "segment", [(i, (i + step) % sections) for i in range(sections)]
            )
        )
    gathered = jnp.stack(gathered)
    by_section = [
        lax.dynamic_index_in_dim(gathered, (segment - s) % sections, 0, keepdims=False)
        for s in range(sections)
    ]

    def arranged(field):
        mine = lax.dynamic_index_in_dim(field, micro, 0, keepdims=False)
        return jnp.transpose(mine, (1, 2, 0, 3)).reshape(planes, rows * channels, across)

    def restored(field):
        return jnp.transpose(
            field.reshape(planes, rows, channels, across), (2, 0, 1, 3)
        )

    merged = arranged(crops)
    outgoing = arranged(cotangent)
    band = (planes, rows * channels, across)
    entering = [merged]
    features, frames, hiddens, slopes1, slopes2 = [], [], [], [], []
    for s in range(sections):
        skip = entering[2 - s] if s in (1, 2) else None
        operands = list(with_halos(merged, channels)) + [by_section[s][0, 0], by_section[s][1, 0]]
        if skip is not None:
            operands.append(skip)
        leaving, merged, wide, hidden, slope1, slope2 = pl.pallas_call(
            functools.partial(forward_kernel, sizes, skip is not None),
            out_shape=(
                bf(*band),
                bf(*band),
                bf(planes, frame, across),
                bf(planes, frame, across),
                fl(planes, inner * channels, across),
                fl(*band),
            ),
            in_specs=[spec] * len(operands),
            out_specs=(spec,) * 6,
            scratch_shapes=[column_scratch, tap_scratch],
            compiler_params=params,
        )(*operands)
        entering.append(leaving)
        features.append(leaving)
        frames.append(wide)
        hiddens.append(hidden)
        slopes1.append(slope1)
        slopes2.append(slope2)

    second = (outgoing.astype(jnp.float32) * slopes2[-1]).astype(jnp.bfloat16)
    seconds = [None] * sections
    firsts = [None] * sections
    grads = [None] * sections
    for s in reversed(range(sections)):
        seconds[s] = second
        operands = list(with_halos(second, channels)) + [
            by_section[s][0, 1],
            by_section[s][1, 1],
            slopes1[s],
        ]
        outs = [bf(*band), bf(*band)]
        if s < 2:
            operands.append(grads[3 - s])
        if s > 0:
            operands.append(slopes2[s - 1])
            outs.append(bf(*band))
        result = pl.pallas_call(
            functools.partial(backward_kernel, sizes, s < 2, s > 0),
            out_shape=tuple(outs),
            in_specs=[spec] * len(operands),
            out_specs=(spec,) * len(outs),
            scratch_shapes=[
                pltpu.VMEM((planes, frame, across), jnp.bfloat16),
                column_scratch,
                tap_scratch,
            ],
            compiler_params=params,
        )(*operands)
        grads[s], firsts[s] = result[0], result[1]
        if s > 0:
            second = result[2]

    def own(values):
        pair = [jnp.where(upper, values[k + 2], values[k]) for k in range(2)]
        keep = jnp.where(micro == 0, pair[0], pair[1])
        give = jnp.where(micro == 0, pair[1], pair[0])
        return keep, give

    def weight_terms(values):
        picked = [jnp.where(upper, values[k + 2], values[k]) for k in range(2)]
        return picked

    picked = [weight_terms(v) for v in (frames, firsts, hiddens, seconds)]
    terms = []
    for k in range(2):
        terms.append(
            pl.pallas_call(
                functools.partial(weight_kernel, sizes),
                out_shape=fl(2, channels, 27 * channels),
                in_specs=[spec] * 4,
                out_specs=spec,
                scratch_shapes=[
                    pltpu.VMEM((27 * channels, planes * rows * across), jnp.bfloat16)
                ],
                compiler_params=params,
            )(*[p[k] for p in picked])
        )
    keep = jnp.where(micro == 0, terms[0], terms[1])
    give = jnp.where(micro == 0, terms[1], terms[0])
    total = keep + partner(give.astype(jnp.bfloat16), "segment", 1).astype(jnp.float32)
    count = lax.axis_size("gy")
    mask = 1
    while mask < count:
        total = total + partner(total.astype(jnp.bfloat16), "gy", mask).astype(jnp.float32)
        mask *= 2
    weight_grads = jnp.transpose(
        total.reshape(2, channels, 27, channels), (0, 2, 3, 1)
    )

    def both(values):
        keep, give = own(values)
        come = partner(give, "segment", 1)
        first = jnp.where(micro == 0, keep, come)
        last = jnp.where(micro == 0, come, keep)
        return jnp.stack([restored(first), restored(last)])

    return (
        both(features)[None],
        weight_grads[None],
        both(grads).astype(jnp.float32)[None],
    )


def solution(mesh):
    return jax.shard_map(
        local,
        mesh=mesh,
        in_specs=(
            P(None, None, None, "gy", None),
            P(None, None, None, "gy", None),
            P("segment", None, None, None, None),
        ),
        out_specs=(
            P("segment", None, None, None, "gy", None),
            P("segment", None, None, None, None),
            P("segment", None, None, None, "gy", None),
        ),
        check_vma=False,
    )
```

```python
import functools

import jax
import jax.numpy as jnp
from jax import lax
from jax.experimental import pallas as pl
from jax.experimental.pallas import tpu as pltpu
from jax.sharding import PartitionSpec as P

HALO = 2


def shifted_fields(value):
    across = value.shape[1]
    lane = lax.broadcasted_iota(jnp.int32, value.shape, 1)
    left = jnp.where(lane == 0, 0.0, pltpu.roll(value, 1, 1))
    right = jnp.where(lane == across - 1, 0.0, pltpu.roll(value, across - 1, 1))
    return [v.astype(jnp.bfloat16) for v in (left, value, right)]


def fill_columns(col, planes_of, planes):
    across = col.shape[-1] // 2
    frame = col.shape[2]
    zero = jnp.zeros((frame, across), jnp.bfloat16)
    for dx in range(3):
        col[dx, 0, :, :across] = zero
        col[dx, planes, :, across:] = zero
    for z in range(planes):
        for dx, field in enumerate(shifted_fields(planes_of(z))):
            col[dx, z + 1, :, :across] = field
            col[dx, z, :, across:] = field


def build_taps(taps, compact, out_rows):
    channels = compact.shape[1]
    frame = taps.shape[2]
    for j in range(9):
        wide = jnp.concatenate(
            [
                compact[j].astype(jnp.float32),
                jnp.zeros((channels, frame - compact.shape[2]), jnp.float32),
            ],
            1,
        )
        for y in range(out_rows):
            moved = wide if y == 0 else pltpu.roll(wide, y * channels, 1)
            taps[j, y * channels : (y + 1) * channels, :] = moved.astype(jnp.bfloat16)


def convolved(taps, col, pair, low, high):
    total = None
    for dz in range(3):
        for dx in range(3):
            part = jnp.dot(
                taps[3 * dz + dx, low:high, :],
                col[dx, 2 * pair + dz],
                preferred_element_type=jnp.float32,
            )
            total = part if total is None else total + part
    return total


def logistic_of(value):
    return 1.0 / (1.0 + jnp.exp(-value))


def row_mask(channels, rows, frame_start, inside_low, inside_high, across):
    row = lax.broadcasted_iota(jnp.int32, (rows * channels, across), 0) // channels + frame_start
    return (row >= inside_low) & (row < inside_high)


def forward_kernel(
    sizes, with_skip, low_ref, mid_ref, high_ref, first_ref, second_ref, *rest
):
    channels, planes, rows, across = sizes
    if with_skip:
        skip_ref, *rest = rest
    (features_ref, next_ref, frame_ref, hidden_ref, slope1_ref, slope2_ref, col, taps) = rest
    gy = lax.axis_index("gy")
    count = lax.axis_size("gy")
    inner = rows + 2
    inside_low = jnp.where(gy == 0, HALO, 0)
    inside_high = jnp.where(gy == count - 1, rows + HALO, rows + 2 * HALO)
    for z in range(planes):
        frame_ref[z, : HALO * channels] = jnp.where(gy == 0, 0.0, low_ref[z].astype(jnp.float32)).astype(jnp.bfloat16)
        frame_ref[z, HALO * channels : (HALO + rows) * channels] = mid_ref[z]
        frame_ref[z, (HALO + rows) * channels :] = jnp.where(gy == count - 1, 0.0, high_ref[z].astype(jnp.float32)).astype(jnp.bfloat16)
    fill_columns(col, lambda z: frame_ref[z].astype(jnp.float32), planes)
    build_taps(taps, first_ref, inner)
    mask = row_mask(channels, inner, 1, inside_low, inside_high, across)
    edge = jnp.zeros((channels, across), jnp.bfloat16)
    for pair in range(planes // 2):
        pre = convolved(taps, col, pair, 0, inner * channels)
        for half in range(2):
            z = 2 * pair + half
            part = pre[:, half * across : (half + 1) * across]
            logistic = logistic_of(part)
            slope1_ref[z] = logistic * (1.0 + part * (1.0 - logistic))
            hidden_ref[z, :channels] = edge
            hidden_ref[z, channels : (inner + 1) * channels] = jnp.where(
                mask, part * logistic, 0.0
            ).astype(jnp.bfloat16)
            hidden_ref[z, (inner + 1) * channels :] = edge
    fill_columns(col, lambda z: hidden_ref[z].astype(jnp.float32), planes)
    build_taps(taps, second_ref, inner)
    for pair in range(planes // 2):
        pre = convolved(taps, col, pair, channels, (rows + 1) * channels)
        for half in range(2):
            z = 2 * pair + half
            part = pre[:, half * across : (half + 1) * across]
            logistic = logistic_of(part)
            slope2_ref[z] = logistic * (1.0 + part * (1.0 - logistic))
            leaving = (part * logistic).astype(jnp.bfloat16)
            features_ref[z] = leaving
            if with_skip:
                leaving = (
                    leaving.astype(jnp.float32) + skip_ref[z].astype(jnp.float32)
                ).astype(jnp.bfloat16)
            next_ref[z] = leaving


def backward_kernel(
    sizes, with_extra, with_next, low_ref, mid_ref, high_ref, first_ref, second_ref, slope1_ref, *rest
):
    channels, planes, rows, across = sizes
    if with_extra:
        extra_ref, *rest = rest
    if with_next:
        slope2_ref, *rest = rest
        (grads_ref, first_delta_ref, next_ref, wide, col, taps) = rest
    else:
        (grads_ref, first_delta_ref, wide, col, taps) = rest
    gy = lax.axis_index("gy")
    count = lax.axis_size("gy")
    inner = rows + 2
    inside_low = jnp.where(gy == 0, HALO, 0)
    inside_high = jnp.where(gy == count - 1, rows + HALO, rows + 2 * HALO)
    for z in range(planes):
        wide[z, : HALO * channels] = jnp.where(gy == 0, 0.0, low_ref[z].astype(jnp.float32)).astype(jnp.bfloat16)
        wide[z, HALO * channels : (HALO + rows) * channels] = mid_ref[z]
        wide[z, (HALO + rows) * channels :] = jnp.where(gy == count - 1, 0.0, high_ref[z].astype(jnp.float32)).astype(jnp.bfloat16)
    fill_columns(col, lambda z: wide[z].astype(jnp.float32), planes)
    build_taps(taps, second_ref, inner)
    mask = row_mask(channels, inner, 1, inside_low, inside_high, across)
    edge = jnp.zeros((channels, across), jnp.bfloat16)
    for pair in range(planes // 2):
        pre = convolved(taps, col, pair, 0, inner * channels)
        for half in range(2):
            z = 2 * pair + half
            part = pre[:, half * across : (half + 1) * across]
            delta = jnp.where(mask, part * slope1_ref[z], 0.0).astype(jnp.bfloat16)
            wide[z, :channels] = edge
            wide[z, channels : (inner + 1) * channels] = delta
            wide[z, (inner + 1) * channels :] = edge
            first_delta_ref[z] = delta[channels : (rows + 1) * channels]
    fill_columns(col, lambda z: wide[z].astype(jnp.float32), planes)
    build_taps(taps, first_ref, inner)
    for pair in range(planes // 2):
        pre = convolved(taps, col, pair, channels, (rows + 1) * channels)
        for half in range(2):
            z = 2 * pair + half
            value = pre[:, half * across : (half + 1) * across].astype(jnp.bfloat16)
            if with_extra:
                value = (
                    value.astype(jnp.float32) + extra_ref[z].astype(jnp.float32)
                ).astype(jnp.bfloat16)
            grads_ref[z] = value
            if with_next:
                next_ref[z] = (value.astype(jnp.float32) * slope2_ref[z]).astype(jnp.bfloat16)


def weight_kernel(sizes, frame_ref, first_ref, hidden_ref, second_ref, out_ref, columns):
    channels, planes, rows, across = sizes
    zero = jnp.zeros((channels, rows * across), jnp.bfloat16)
    for index, (source, delta) in enumerate(((frame_ref, first_ref), (hidden_ref, second_ref))):
        for z in range(planes):
            fields = shifted_fields(source[z].astype(jnp.float32))
            for dx, field in enumerate(fields):
                for dy in range(3):
                    block = jnp.concatenate(
                        [
                            field[(y + 1 + dy) * channels : (y + 2 + dy) * channels]
                            for y in range(rows)
                        ],
                        1,
                    )
                    for dz in range(3):
                        target = z + 1 - dz
                        if 0 <= target < planes:
                            tap = (9 * dz + 3 * dy + dx) * channels
                            columns[
                                tap : tap + channels,
                                target * rows * across : (target + 1) * rows * across,
                            ] = block
        for dz, target in ((0, 0), (2, planes - 1)):
            for tap in range(9 * dz, 9 * dz + 9):
                columns[
                    tap * channels : (tap + 1) * channels,
                    target * rows * across : (target + 1) * rows * across,
                ] = zero
        right = jnp.concatenate(
            [
                delta[z, y * channels : (y + 1) * channels, :]
                for z in range(planes)
                for y in range(rows)
            ],
            1,
        )
        out_ref[index] = lax.dot_general(
            right, columns[...], (((1,), (1,)), ((), ())), preferred_element_type=jnp.float32
        )


def exchange_kernel(block_ref, low_ref, high_ref, send_sem, recv_sem):
    count = lax.axis_size("gy")
    me = lax.axis_index("gy")
    after, before = lax.rem(me + 1, count), lax.rem(me + count - 1, count)
    barrier = pltpu.get_barrier_semaphore()
    for neighbour in (before, after):
        pl.semaphore_signal(
            barrier, inc=1, device_id={"gy": neighbour}, device_id_type=pl.DeviceIdType.MESH
        )
    pl.semaphore_wait(barrier, 2)
    width = low_ref.shape[1]
    last = block_ref.shape[1] - width
    copies = [
        pltpu.make_async_remote_copy(
            src_ref=block_ref.at[:, pl.ds(start, width), :],
            dst_ref=target,
            send_sem=send_sem.at[k],
            recv_sem=recv_sem.at[k],
            device_id={"gy": neighbour},
            device_id_type=pl.DeviceIdType.MESH,
        )
        for k, (start, target, neighbour) in enumerate(
            ((last, low_ref, after), (0, high_ref, before))
        )
    ]
    for copy in copies:
        copy.start()
    for copy in copies:
        copy.wait()


def with_halos(block, channels):
    width = HALO * channels
    halo = jax.ShapeDtypeStruct((block.shape[0], width, block.shape[2]), block.dtype)
    spec = pl.BlockSpec(memory_space=pltpu.VMEM)
    low, high = pl.pallas_call(
        exchange_kernel,
        out_shape=(halo, halo),
        in_specs=[spec],
        out_specs=(spec, spec),
        scratch_shapes=[pltpu.SemaphoreType.DMA((2,)), pltpu.SemaphoreType.DMA((2,))],
        compiler_params=pltpu.CompilerParams(collective_id=0, has_side_effects=True),
    )(block)
    return low, block, high


def partner(array, axis, mask):
    return lax.ppermute(array, axis, [(i, i ^ mask) for i in range(lax.axis_size(axis))])


def local(crops, cotangent, weights):
    micro_count, channels, planes, rows, across = crops.shape
    sizes = (channels, planes, rows, across)
    segment = lax.axis_index("segment")
    sections = lax.axis_size("segment")
    micro = segment % 2
    upper = segment >= 2
    inner = rows + 2
    frame = (rows + 2 * HALO) * channels
    spec = pl.BlockSpec(memory_space=pltpu.VMEM)
    bf = lambda *shape: jax.ShapeDtypeStruct(shape, jnp.bfloat16)
    fl = lambda *shape: jax.ShapeDtypeStruct(shape, jnp.float32)
    params = pltpu.CompilerParams(vmem_limit_bytes=48 * 2**20)
    column_scratch = pltpu.VMEM((3, planes + 1, frame, 2 * across), jnp.bfloat16)
    tap_scratch = pltpu.VMEM((9, inner * channels, frame), jnp.bfloat16)

    kernels = weights[0].reshape(2, 3, 3, 3, channels, channels)
    straight = jnp.transpose(kernels, (0, 1, 3, 5, 2, 4))
    turned = jnp.transpose(jnp.flip(kernels, (1, 2, 3)), (0, 1, 3, 4, 2, 5))
    compact = jnp.stack([straight, turned], 1).reshape(2, 2, 9, channels, 3 * channels)
    compact = jnp.pad(compact, ((0, 0),) * 4 + ((0, 128 - 3 * channels),))
    gathered = [compact]
    for step in range(1, sections):
        gathered.append(
            lax.ppermute(
                compact, "segment", [(i, (i + step) % sections) for i in range(sections)]
            )
        )
    gathered = jnp.stack(gathered)
    by_section = [
        lax.dynamic_index_in_dim(gathered, (segment - s) % sections, 0, keepdims=False)
        for s in range(sections)
    ]

    def arranged(field):
        mine = lax.dynamic_index_in_dim(field, micro, 0, keepdims=False)
        return jnp.transpose(mine, (1, 2, 0, 3)).reshape(planes, rows * channels, across)

    def restored(field):
        return jnp.transpose(
            field.reshape(planes, rows, channels, across), (2, 0, 1, 3)
        )

    merged = arranged(crops)
    outgoing = arranged(cotangent)
    band = (planes, rows * channels, across)
    entering = [merged]
    features, frames, hiddens, slopes1, slopes2 = [], [], [], [], []
    for s in range(sections):
        skip = entering[2 - s] if s in (1, 2) else None
        operands = list(with_halos(merged, channels)) + [by_section[s][0, 0], by_section[s][1, 0]]
        if skip is not None:
            operands.append(skip)
        leaving, merged, wide, hidden, slope1, slope2 = pl.pallas_call(
            functools.partial(forward_kernel, sizes, skip is not None),
            out_shape=(
                bf(*band),
                bf(*band),
                bf(planes, frame, across),
                bf(planes, frame, across),
                fl(planes, inner * channels, across),
                fl(*band),
            ),
            in_specs=[spec] * len(operands),
            out_specs=(spec,) * 6,
            scratch_shapes=[column_scratch, tap_scratch],
            compiler_params=params,
        )(*operands)
        entering.append(leaving)
        features.append(leaving)
        frames.append(wide)
        hiddens.append(hidden)
        slopes1.append(slope1)
        slopes2.append(slope2)

    second = (outgoing.astype(jnp.float32) * slopes2[-1]).astype(jnp.bfloat16)
    seconds = [None] * sections
    firsts = [None] * sections
    grads = [None] * sections
    for s in reversed(range(sections)):
        seconds[s] = second
        operands = list(with_halos(second, channels)) + [
            by_section[s][0, 1],
            by_section[s][1, 1],
            slopes1[s],
        ]
        outs = [bf(*band), bf(*band)]
        if s < 2:
            operands.append(grads[3 - s])
        if s > 0:
            operands.append(slopes2[s - 1])
            outs.append(bf(*band))
        result = pl.pallas_call(
            functools.partial(backward_kernel, sizes, s < 2, s > 0),
            out_shape=tuple(outs),
            in_specs=[spec] * len(operands),
            out_specs=(spec,) * len(outs),
            scratch_shapes=[
                pltpu.VMEM((planes, frame, across), jnp.bfloat16),
                column_scratch,
                tap_scratch,
            ],
            compiler_params=params,
        )(*operands)
        grads[s], firsts[s] = result[0], result[1]
        if s > 0:
            second = result[2]

    def own(values):
        pair = [jnp.where(upper, values[k + 2], values[k]) for k in range(2)]
        keep = jnp.where(micro == 0, pair[0], pair[1])
        give = jnp.where(micro == 0, pair[1], pair[0])
        return keep, give

    def weight_terms(values):
        picked = [jnp.where(upper, values[k + 2], values[k]) for k in range(2)]
        return picked

    picked = [weight_terms(v) for v in (frames, firsts, hiddens, seconds)]
    terms = []
    for k in range(2):
        terms.append(
            pl.pallas_call(
                functools.partial(weight_kernel, sizes),
                out_shape=fl(2, channels, 27 * channels),
                in_specs=[spec] * 4,
                out_specs=spec,
                scratch_shapes=[
                    pltpu.VMEM((27 * channels, planes * rows * across), jnp.bfloat16)
                ],
                compiler_params=params,
            )(*[p[k] for p in picked])
        )
    keep = jnp.where(micro == 0, terms[0], terms[1])
    give = jnp.where(micro == 0, terms[1], terms[0])
    total = keep + partner(give.astype(jnp.bfloat16), "segment", 1).astype(jnp.float32)
    count = lax.axis_size("gy")
    mask = 1
    while mask < count:
        total = total + partner(total.astype(jnp.bfloat16), "gy", mask).astype(jnp.float32)
        mask *= 2
    weight_grads = jnp.transpose(
        total.reshape(2, channels, 27, channels), (0, 2, 3, 1)
    )

    def both(values):
        keep, give = own(values)
        come = partner(give, "segment", 1)
        first = jnp.where(micro == 0, keep, come)
        last = jnp.where(micro == 0, come, keep)
        return jnp.stack([restored(first), restored(last)])

    return (
        both(features)[None],
        weight_grads[None],
        both(grads).astype(jnp.float32)[None],
    )


def solution(mesh):
    return jax.shard_map(
        local,
        mesh=mesh,
        in_specs=(
            P(None, None, None, "gy", None),
            P(None, None, None, "gy", None),
            P("segment", None, None, None, None),
        ),
        out_specs=(
            P("segment", None, None, None, "gy", None),
            P("segment", None, None, None, None),
            P("segment", None, None, None, "gy", None),
        ),
        check_vma=False,
    )
```
